32 devices in a mesh: row: 8 (over y, x, core), col: 4 (over z).
Axes of the slice: x: 2, y: 2, z: 4, core: 2. Of those that a mesh axis runs over, the one named last changes fastest.
Arguments:
- tile_values: bfloat16 [8, 4, 64, 128, 128], P('row', 'col'), may hold values from -0.0625 to 0.0625
- tile_row: int32 [8, 4, 64], P('row', 'col'), may hold values from 0 to 3
- tile_col: int32 [8, 4, 64], P('row', 'col'), may hold values from 0 to 3
- tile_count: int32 [8, 4], P('row', 'col'), may hold values from 16 to 64, as said below
- primal_init: float32 [64, 2048], P(None, ('row', 'col')), may hold values from -3 to 3
- dual_init: float32 [64, 4096], P(None, ('row', 'col')), may hold values from -3 to 3
- cost_vector: float32 [2048], P(('row', 'col')), may hold values from -4 to 4
- lower_bound: float32 [2048], P(('row', 'col')), may hold values from -1 to -0.2
- upper_bound: float32 [2048], P(('row', 'col')), may hold values from 0.2 to 1
- bound_kind: int32 [2048], P(('row', 'col')), may hold values from 0 to 2
- row_kind: int32 [4096], P(('row', 'col')), may hold values from 0 to 1
- demand: float32 [64, 4096], P(None, ('row', 'col')), may hold values from -20 to 20
Outputs:
- primal_out: float32 [64, 2048], P(None, ('row', 'col'))
- dual_out: float32 [64, 4096], P(None, ('row', 'col'))
- residual_norm: float32 [3, 64], replicated
The draws below stay inside these ranges and needn't reach their ends.
Inputs may be any that keep to these rules, and one draw needn't show every extreme that they name: `tile_count`: live tile slots of one device; some device has all 64 slots live.
All inputs are finite; a program needn't handle non-finite values.
Results may differ from the reference program's by a relative error of at most 0.0022.
Values may be sent and summed in bfloat16 or wider, within the bound.
A program may use at most 64 MiB of HBM per device.

```python
import jax
import jax.numpy as jnp
from jax import lax

TILE = 128
SCEN = 64
TCAP = 64
ITERS = 3
VAR_DEV = 64
NCOL = 2048
NROWS = 4096
N_ROW = 8
N_COL = 4


def draw_tile_count(key, part):
    first_key, second_key = jax.random.split(key)
    total_lists = N_ROW * N_COL
    counts = jax.random.randint(first_key, (total_lists,), max(TCAP // 4, 1), TCAP + 1)
    chosen = jax.random.randint(second_key, (), 0, total_lists)
    counts = jnp.where(jnp.arange(total_lists) == chosen, TCAP, counts)
    return counts.reshape(N_ROW, N_COL).astype(jnp.int32)


def draw_demand(key, part):
    row_place = jnp.arange(NROWS, dtype=jnp.float32) / NROWS
    scen_place = jnp.arange(SCEN, dtype=jnp.float32) / SCEN
    scale = 0.5 * (10.0 ** (0.5 * row_place))[None, :] * (10.0 ** (0.5 * scen_place))[:, None]
    base = jnp.clip(jax.random.normal(key, (SCEN, NROWS), jnp.float32), -4.0, 4.0)
    return (base * scale).astype(jnp.float32)


def touch_ends(result, stream_key, low, top_value):
    place = [jax.random.randint(jax.random.fold_in(stream_key, axis), (), 0, length) for axis, length in enumerate(result.shape)]
    main_axis = result.shape.index(max(result.shape))
    beside = place[:main_axis] + [(place[main_axis] + 1) % result.shape[main_axis]] + place[main_axis + 1:]
    return result.at[tuple(place)].set(low).at[tuple(beside)].set(top_value)


def shard_levels(stream_key, dims, shards, least, largest):
    gain = 1.0
    for position, shards_of in shards:
        steps = jax.random.uniform(jax.random.fold_in(jax.random.fold_in(stream_key, 6), position), (shards_of,), jnp.float32, least / len(shards), largest / len(shards))
        gain = gain * jnp.repeat(jnp.exp(steps), dims[position] // shards_of).reshape((-1,) + (1,) * (len(dims) - 1 - position))
    return gain


def noise(stream_key, shape, deviation, most, cuts=(), kind=jnp.bfloat16):
    values = deviation * jax.random.normal(stream_key, shape, jnp.float32)
    if cuts:
        values = values * shard_levels(stream_key, shape, cuts, -0.22, 0.18)
    return jnp.clip(values, -most, most).astype(kind)


def setup_inputs(seed: int = 0) -> dict:
    splits = jax.random.split(jax.random.key(seed), 13)
    return {
        "tile_values": noise(splits[0], (N_ROW, N_COL, TCAP, TILE, TILE), (TILE * TCAP) ** -0.5, 0.0625, ((0, 8), (1, 4))),
        "tile_row": touch_ends(jax.random.randint(splits[1], (N_ROW, N_COL, TCAP), 0, N_COL), jax.random.fold_in(splits[1], 1), 0, N_COL - 1).astype(jnp.int32),
        "tile_col": touch_ends(jax.random.randint(splits[2], (N_ROW, N_COL, TCAP), 0, N_ROW // 2), jax.random.fold_in(splits[2], 1), 0, (N_ROW // 2) - 1).astype(jnp.int32),
        "tile_count": draw_tile_count(jax.random.fold_in(splits[12], 71), 0),
        "primal_init": noise(splits[4], (SCEN, NCOL), 0.5, 3.0, ((1, 32),), jnp.float32),
        "dual_init": noise(splits[5], (SCEN, NROWS), 0.5, 3.0, ((1, 32),), jnp.float32),
        "cost_vector": noise(splits[6], (NCOL,), 1.0, 4.0, ((0, 32),), jnp.float32),
        "lower_bound": jnp.clip(-1.0 + 0.8 * jax.random.uniform(splits[7], (NCOL,), jnp.float32) ** shard_levels(splits[7], (NCOL,), ((0, 32),), -0.2, 0.2), -1.0, -0.2),
        "upper_bound": jnp.clip(0.2 + 0.8 * jax.random.uniform(splits[8], (NCOL,), jnp.float32) ** shard_levels(splits[8], (NCOL,), ((0, 32),), -0.2, 0.2), 0.2, 1.0),
        "bound_kind": touch_ends(jax.random.randint(splits[9], (NCOL,), 0, 3), jax.random.fold_in(splits[9], 1), 0, 2).astype(jnp.int32),
        "row_kind": touch_ends(jax.random.randint(splits[10], (NROWS,), 0, 2), jax.random.fold_in(splits[10], 1), 0, 1).astype(jnp.int32),
        "demand": draw_demand(jax.random.fold_in(splits[12], 71), 0),
    }


def project_primal(values, lower_bound, upper_bound, bound_kind):
    values = jnp.where((bound_kind <= 1)[None, :], jnp.maximum(values, lower_bound[None, :]), values)
    values = jnp.where((bound_kind == 0)[None, :], jnp.minimum(values, upper_bound[None, :]), values)
    return values

def reference(tile_values, tile_row, tile_col, tile_count, primal_init, dual_init, cost_vector, lower_bound, upper_bound, bound_kind, row_kind, demand):
    devices_all = N_ROW * N_COL
    col_blocks = N_ROW // 2
    flat_tiles = tile_values.reshape(devices_all, TCAP, TILE, TILE)
    flat_rows = tile_row.reshape(devices_all, TCAP)
    flat_cols = tile_col.reshape(devices_all, TCAP)
    flat_count = tile_count.reshape(devices_all)
    device_ids = jnp.arange(devices_all, dtype=jnp.int32)
    slot_ids = jnp.arange(TCAP, dtype=jnp.int32)
    row_ids = jnp.arange(N_COL, dtype=jnp.int32)
    col_ids = jnp.arange(col_blocks, dtype=jnp.int32)

    def apply_forward(extrapolated):
        grouped = extrapolated.reshape(SCEN, col_blocks, 2, N_COL, VAR_DEV)
        grouped = grouped.transpose(3, 1, 0, 2, 4).reshape(N_COL, col_blocks, SCEN, TILE)

        def visit(total, item):
            blocks, rows, cols, count, device = item
            row_index = device // N_COL
            col_index = device % N_COL
            live_mask = (slot_ids < count).astype(jnp.float32)
            picked = grouped[col_index][cols].astype(jnp.float32)
            product = jnp.einsum('tij,tsj->tsi', blocks.astype(jnp.float32), picked, precision=lax.Precision.HIGHEST)
            onehot = (rows[:, None] == row_ids[None, :]).astype(jnp.float32) * live_mask[:, None]
            summed = jnp.einsum('tr,tsi->rsi', onehot, product, precision=lax.Precision.HIGHEST)
            return (total.at[row_index].add(summed), None)
        start = jnp.zeros((N_ROW, N_COL, SCEN, TILE), jnp.float32)
        total, _ = lax.scan(visit, start, (flat_tiles, flat_rows, flat_cols, flat_count, device_ids))
        return total.transpose(2, 0, 1, 3).reshape(SCEN, NROWS)

    def apply_backward(dual_half):
        grouped = dual_half.reshape(SCEN, N_ROW, N_COL, TILE).transpose(1, 2, 0, 3)

        def visit(total, item):
            blocks, rows, cols, count, device = item
            row_index = device // N_COL
            col_index = device % N_COL
            live_mask = (slot_ids < count).astype(jnp.float32)
            picked = grouped[row_index][rows].astype(jnp.float32)
            product = jnp.einsum('tij,tsi->tsj', blocks.astype(jnp.float32), picked, precision=lax.Precision.HIGHEST)
            onehot = (cols[:, None] == col_ids[None, :]).astype(jnp.float32) * live_mask[:, None]
            summed = jnp.einsum('tc,tsj->csj', onehot, product, precision=lax.Precision.HIGHEST)
            return (total.at[col_index].add(summed), None)
        start = jnp.zeros((N_COL, col_blocks, SCEN, TILE), jnp.float32)
        total, _ = lax.scan(visit, start, (flat_tiles, flat_rows, flat_cols, flat_count, device_ids))
        total = total.reshape(N_COL, col_blocks, SCEN, 2, VAR_DEV)
        return total.transpose(2, 1, 3, 0, 4).reshape(SCEN, NCOL)
    primal = primal_init
    dual = dual_init
    norms = []
    for iteration in range(ITERS):
        dual_half = dual.astype(jnp.bfloat16)
        transposed = apply_backward(dual_half)
        primal_next = primal - 0.4 * (cost_vector[None, :] - transposed)
        primal_next = project_primal(primal_next, lower_bound, upper_bound, bound_kind)
        extrapolated = (2.0 * primal_next - primal).astype(jnp.bfloat16)
        image = apply_forward(extrapolated)
        gap_rows = demand - image
        dual = dual + 0.4 * gap_rows
        dual = jnp.where((row_kind == 1)[None, :], jnp.maximum(dual, 0.0), dual)
        primal = primal_next
        norms.append(jnp.sqrt(lax.optimization_barrier(jnp.sum(gap_rows * gap_rows, axis=1)) / NROWS + 1e-06))
    return (primal, dual, jnp.stack(norms))
```

```python
import functools
import math

import jax
import jax.numpy as jnp
from jax import lax
from jax.experimental import pallas as pl
from jax.experimental.pallas import tpu as pltpu
from jax.sharding import PartitionSpec as P

ITERS = 3
PRIMAL_STEP = 0.4
DUAL_STEP = 0.4
NORM_EPS = 1e-06
MESH = pl.DeviceIdType.MESH
CHUNK = 512
VMEM_LIMIT = 56 * 1024 * 1024


def dense_kernel(rows_ref, cols_ref, count_ref, tiles_ref, hi_ref, lo_ref, acc):
    tile = tiles_ref.shape[-1]
    acc[...] = jnp.zeros_like(acc)

    def add(slot, carry):
        r = pl.multiple_of(rows_ref[0, 0, slot] * tile, tile)
        c = pl.multiple_of(cols_ref[0, 0, slot] * tile, tile)
        where = (pl.ds(r, tile), pl.ds(c, tile))
        acc[where] += tiles_ref[0, 0, slot].astype(jnp.float32)
        return carry

    lax.fori_loop(0, count_ref[0, 0], add, 0)

    def split(block, carry):
        where = (pl.ds(pl.multiple_of(block * tile, tile), tile), slice(None))
        whole = acc[where]
        hi = whole.astype(jnp.bfloat16)
        hi_ref[where] = hi
        lo_ref[where] = (whole - hi.astype(jnp.float32)).astype(jnp.bfloat16)
        return carry

    lax.fori_loop(0, acc.shape[0] // tile, split, 0)


def step_kernel(
    n_row,
    n_col,
    hi_ref,
    lo_ref,
    primal_ref,
    dual_ref,
    cost_ref,
    lower_ref,
    upper_ref,
    bound_ref,
    kind_ref,
    demand_ref,
    primal_out,
    dual_out,
    norm_out,
    duals,
    back_part,
    back_recv,
    points,
    fwd_part,
    fwd_recv,
    swap_send,
    swap_recv,
    fin_send,
    fin_recv,
    norm_row,
    norm_col,
    send_sem,
    recv_sem,
):
    me_r = lax.axis_index("row")
    me_c = lax.axis_index("col")
    block = me_r // 2
    half = lax.rem(me_r, 2)
    scen, tile = dual_ref.shape
    part = scen // 2
    width = primal_ref.shape[1]
    sibling = me_r + 1 - 2 * half

    barrier = pltpu.get_barrier_semaphore()
    for k in range(1, n_row):
        pl.semaphore_signal(
            barrier, inc=1, device_id={"row": lax.rem(me_r + k, n_row)}, device_id_type=MESH
        )
    for k in range(1, n_col):
        pl.semaphore_signal(
            barrier, inc=1, device_id={"col": lax.rem(me_c + k, n_col)}, device_id_type=MESH
        )

    def lanes(index):
        return pl.ds(pl.multiple_of(index * tile, tile), tile)

    def scens(index):
        return pl.ds(pl.multiple_of(index * part, part), part)

    def send(src, dst, sem, target):
        copy = pltpu.make_async_remote_copy(
            src_ref=src,
            dst_ref=dst,
            send_sem=send_sem.at[sem],
            recv_sem=recv_sem.at[sem],
            device_id=target,
            device_id_type=MESH,
        )
        copy.start()
        return copy

    dims = (((1,), (1,)), ((), ()))

    def multiply(left, out, flip):
        deep, wide = left.shape[1], out.shape[1]
        step, span = math.gcd(deep, CHUNK), math.gcd(wide, CHUNK)

        def term(d, w):
            x = left[:, d]
            if flip:
                return lax.dot_general(
                    x, hi_ref[w, d], dims, preferred_element_type=jnp.float32
                ) + lax.dot_general(x, lo_ref[w, d], dims, preferred_element_type=jnp.float32)
            return jnp.dot(x, hi_ref[d, w], preferred_element_type=jnp.float32) + jnp.dot(
                x, lo_ref[d, w], preferred_element_type=jnp.float32
            )

        if step == deep and span == wide:
            out[...] = term(slice(None), slice(None))
            return

        def column(j, carry):
            w = pl.ds(pl.multiple_of(j * span, span), span)

            def add(i, total):
                return total + term(pl.ds(pl.multiple_of(i * step, step), step), w)

            out[:, w] = lax.fori_loop(0, deep // step, add, jnp.zeros((scen, span), jnp.float32))
            return carry

        lax.fori_loop(0, wide // span, column, 0)

    started = []
    next_sem = [0]

    def sem():
        next_sem[0] += 1
        return next_sem[0] - 1

    def row_peer(k):
        return lax.rem(me_r + k, n_row)

    def col_peer(k):
        return lax.rem(me_c + k, n_col)

    def finish(copies):
        for copy in copies:
            copy.wait_recv()
        started.extend(copies)

    dual = dual_ref[...]
    duals[0, :, lanes(me_c)] = dual.astype(jnp.bfloat16)
    kind = bound_ref[...].reshape(1, width)
    cost_own = cost_ref[...].reshape(1, width)
    lower_own = jnp.where(kind <= 1, lower_ref[...].reshape(1, width), -jnp.inf)
    upper_own = jnp.where(kind == 0, upper_ref[...].reshape(1, width), jnp.inf)
    swap_send[...] = jnp.zeros_like(swap_send)
    swap_send[0:part, 0:width] = primal_ref[scens(1 - half), :]
    swap_send[part : part + 1, 0:width] = cost_own
    swap_send[part + 1 : part + 2, 0:width] = lower_own
    swap_send[part + 2 : part + 3, 0:width] = upper_own
    inequality = kind_ref[...].reshape(1, tile) == 1
    norm_row[me_r] = jnp.zeros(norm_row.shape[1:], jnp.float32)

    pl.semaphore_wait(barrier, n_row + n_col - 2)

    swap = None
    for it in range(ITERS):
        copies = []
        for k in range(1, n_col):
            mine = duals.at[it, :, lanes(me_c)]
            copies.append(send(mine, mine, sem(), {"col": col_peer(k)}))
        if it == 0:
            swap = send(swap_send, swap_recv, sem(), {"row": sibling})
        finish(copies)

        multiply(duals.at[it], back_part.at[it], False)
        copies = []
        for k in range(1, n_row):
            peer = row_peer(k)
            source = back_part.at[it, scens(lax.rem(peer, 2)), lanes(peer // 2)]
            copies.append(send(source, back_recv.at[it, k - 1], sem(), {"row": peer}))
        if it == 0:
            finish([swap])
            first = half == 0

            def pair(own, other):
                return jnp.where(
                    first,
                    jnp.concatenate([own, other], axis=1),
                    jnp.concatenate([other, own], axis=1),
                )

            primal = pair(primal_ref[scens(half), :], swap_recv[0:part, 0:width])
            cost = pair(cost_own, swap_recv[part : part + 1, 0:width])
            lower = pair(lower_own, swap_recv[part + 1 : part + 2, 0:width])
            upper = pair(upper_own, swap_recv[part + 2 : part + 3, 0:width])
        transposed = back_part[it, scens(half), lanes(block)]
        finish(copies)
        for k in range(1, n_row):
            transposed = transposed + back_recv[it, k - 1]

        moved = primal - PRIMAL_STEP * (cost - transposed)
        moved = jnp.minimum(jnp.maximum(moved, lower), upper)
        points[it, scens(half), lanes(block)] = (2.0 * moved - primal).astype(jnp.bfloat16)
        primal = moved
        copies = []
        for k in range(1, n_row):
            mine = points.at[it, scens(half), lanes(block)]
            copies.append(send(mine, mine, sem(), {"row": row_peer(k)}))
        last = None
        if it == ITERS - 1:
            low, high = primal[:, 0:width], primal[:, width:]
            fin_send[:, 0:width] = jnp.where(first, high, low)
            fin_send[:, width:] = jnp.zeros((part, tile - width), jnp.float32)
            last = send(fin_send, fin_recv, sem(), {"row": sibling})
            primal_out[scens(half), :] = jnp.where(first, low, high)
        finish(copies)

        multiply(points.at[it], fwd_part.at[it], True)
        copies = []
        for k in range(1, n_col):
            peer = col_peer(k)
            source = fwd_part.at[it, :, lanes(peer)]
            copies.append(send(source, fwd_recv.at[it, k - 1], sem(), {"col": peer}))
        if last is not None:
            finish([last])
            primal_out[scens(1 - half), :] = fin_recv[:, 0:width]
        image = fwd_part[it, :, lanes(me_c)]
        finish(copies)
        for k in range(1, n_col):
            image = image + fwd_recv[it, k - 1]

        gap = demand_ref[...] - image
        dual = dual + DUAL_STEP * gap
        dual = jnp.where(inequality, jnp.maximum(dual, 0.0), dual)
        if it < ITERS - 1:
            duals[it + 1, :, lanes(me_c)] = dual.astype(jnp.bfloat16)
        else:
            dual_out[...] = dual
        squares = lax.dot_general(
            jnp.ones((8, tile), jnp.float32),
            gap * gap,
            dims,
            precision=lax.Precision.HIGHEST,
            preferred_element_type=jnp.float32,
        )
        norm_row[me_r, it : it + 1, 0:scen] = squares[0:1]

    copies = []
    for k in range(1, n_row):
        mine = norm_row.at[me_r]
        copies.append(send(mine, mine, sem(), {"row": row_peer(k)}))
    finish(copies)
    total = norm_row[0]
    for r in range(1, n_row):
        total = total + norm_row[r]
    norm_col[me_c] = total
    copies = []
    for k in range(1, n_col):
        mine = norm_col.at[me_c]
        copies.append(send(mine, mine, sem(), {"col": col_peer(k)}))
    finish(copies)
    total = norm_col[0]
    for c in range(1, n_col):
        total = total + norm_col[c]
    rows = n_row * n_col * tile
    norm_out[...] = jnp.sqrt(total[0:ITERS, 0:scen] / rows + NORM_EPS)
    for copy in started:
        copy.wait_send()


def shards(
    tile_values,
    tile_row,
    tile_col,
    tile_count,
    primal_init,
    dual_init,
    cost_vector,
    lower_bound,
    upper_bound,
    bound_kind,
    row_kind,
    demand,
):
    n_row = lax.axis_size("row")
    n_col = lax.axis_size("col")
    tile = tile_values.shape[-1]
    scen, width = primal_init.shape
    part = scen // 2
    rows, cols = n_col * tile, (n_row // 2) * tile
    vmem = pl.BlockSpec(memory_space=pltpu.VMEM)
    smem = pl.BlockSpec(memory_space=pltpu.SMEM)
    half_type = jax.ShapeDtypeStruct((rows, cols), jnp.bfloat16)
    hi, lo = pl.pallas_call(
        dense_kernel,
        out_shape=(half_type, half_type),
        in_specs=[smem, smem, smem, vmem],
        out_specs=(vmem, vmem),
        scratch_shapes=[pltpu.VMEM((rows, cols), jnp.float32)],
        compiler_params=pltpu.CompilerParams(vmem_limit_bytes=VMEM_LIMIT),
    )(tile_row, tile_col, tile_count, tile_values)
    sems = ITERS * 2 * (n_row + n_col - 2) + n_row + n_col
    f32, bf16 = jnp.float32, jnp.bfloat16
    return pl.pallas_call(
        functools.partial(step_kernel, n_row, n_col),
        out_shape=(
            jax.ShapeDtypeStruct((scen, width), f32),
            jax.ShapeDtypeStruct((scen, tile), f32),
            jax.ShapeDtypeStruct((ITERS, scen), f32),
        ),
        in_specs=[vmem] * 10,
        out_specs=(vmem, vmem, vmem),
        scratch_shapes=[
            pltpu.VMEM((ITERS, scen, rows), bf16),
            pltpu.VMEM((ITERS, scen, cols), f32),
            pltpu.VMEM((ITERS, n_row - 1, part, tile), f32),
            pltpu.VMEM((ITERS, scen, cols), bf16),
            pltpu.VMEM((ITERS, scen, rows), f32),
            pltpu.VMEM((ITERS, n_col - 1, scen, tile), f32),
            pltpu.VMEM((part + 8, tile), f32),
            pltpu.VMEM((part + 8, tile), f32),
            pltpu.VMEM((part, tile), f32),
            pltpu.VMEM((part, tile), f32),
            pltpu.VMEM((n_row, 8, tile), f32),
            pltpu.VMEM((n_col, 8, tile), f32),
            pltpu.SemaphoreType.DMA((sems,)),
            pltpu.SemaphoreType.DMA((sems,)),
        ],
        compiler_params=pltpu.CompilerParams(
            collective_id=0, has_side_effects=True, vmem_limit_bytes=VMEM_LIMIT
        ),
    )(
        hi,
        lo,
        primal_init,
        dual_init,
        cost_vector,
        lower_bound,
        upper_bound,
        bound_kind,
        row_kind,
        demand,
    )


def solution(mesh):
    return jax.shard_map(
        shards,
        mesh=mesh,
        in_specs=(
            P("row", "col", None, None, None),
            P("row", "col", None),
            P("row", "col", None),
            P("row", "col"),
            P(None, ("row", "col")),
            P(None, ("row", "col")),
            P(("row", "col")),
            P(("row", "col")),
            P(("row", "col")),
            P(("row", "col")),
            P(("row", "col")),
            P(None, ("row", "col")),
        ),
        out_specs=(P(None, ("row", "col")), P(None, ("row", "col")), P()),
        check_vma=False,
    )
```

```python
import functools
import math

import jax
import jax.numpy as jnp
from jax import lax
from jax.experimental import pallas as pl
from jax.experimental.pallas import tpu as pltpu
from jax.sharding import PartitionSpec as P

ITERS = 3
PRIMAL_STEP = 0.4
DUAL_STEP = 0.4
NORM_EPS = 1e-06
MESH = pl.DeviceIdType.MESH
CHUNK = 1024
BACK_TYPE = jnp.bfloat16
FWD_TYPE = jnp.bfloat16
VMEM_LIMIT = 56 * 1024 * 1024


def dense_kernel(rows_ref, cols_ref, count_ref, tiles_ref, hi_ref, lo_ref, acc):
    tile = tiles_ref.shape[-1]
    acc[...] = jnp.zeros_like(acc)

    def add(slot, carry):
        r = pl.multiple_of(rows_ref[0, 0, slot] * tile, tile)
        c = pl.multiple_of(cols_ref[0, 0, slot] * tile, tile)
        where = (pl.ds(r, tile), pl.ds(c, tile))
        acc[where] += tiles_ref[0, 0, slot].astype(jnp.float32)
        return carry

    lax.fori_loop(0, count_ref[0, 0], add, 0)

    def split(block, carry):
        where = (pl.ds(pl.multiple_of(block * tile, tile), tile), slice(None))
        whole = acc[where]
        hi = whole.astype(jnp.bfloat16)
        hi_ref[where] = hi
        lo_ref[where] = (whole - hi.astype(jnp.float32)).astype(jnp.bfloat16)
        return carry

    lax.fori_loop(0, acc.shape[0] // tile, split, 0)


def step_kernel(
    n_row,
    n_col,
    hi_ref,
    lo_ref,
    primal_ref,
    dual_ref,
    cost_ref,
    lower_ref,
    upper_ref,
    bound_ref,
    kind_ref,
    demand_ref,
    primal_out,
    dual_out,
    norm_out,
    full_hi,
    full_lo,
    var_send,
    var_recv,
    con_send,
    con_recv,
    dual_half,
    point,
    back_recv,
    fwd_recv,
    held,
    held_dual,
    fin_send,
    fin_recv,
    fin_dual,
    norm_row,
    local_sem,
    send_sem,
    recv_sem,
):
    me_r = lax.axis_index("row")
    me_c = lax.axis_index("col")
    chips = n_row // 2
    chip = me_r // 2
    half = lax.rem(me_r, 2)
    scen, tile = dual_ref.shape
    part = scen // 2
    width = primal_ref.shape[1]
    rows, cols = hi_ref.shape
    sibling = me_r + 1 - 2 * half

    def row_peer(k):
        return lax.rem(me_r + k, n_row)

    def col_peer(k):
        return lax.rem(me_c + k, n_col)

    barrier = pltpu.get_barrier_semaphore()
    for k in range(1, n_row):
        pl.semaphore_signal(
            barrier, inc=1, device_id={"row": row_peer(k), "col": me_c}, device_id_type=MESH
        )
    for k in range(1, n_col):
        for r in (me_r, sibling):
            pl.semaphore_signal(
                barrier, inc=1, device_id={"row": r, "col": col_peer(k)}, device_id_type=MESH
            )
    loads = [
        pltpu.make_async_copy(hi_ref, full_hi.at[0:rows], local_sem.at[0]),
        pltpu.make_async_copy(lo_ref, full_lo.at[0:rows], local_sem.at[1]),
    ]
    for load in loads:
        load.start()

    def lanes(index, offset=0):
        return pl.ds(pl.multiple_of(index * tile + offset, tile), tile)

    def scens(index):
        return pl.ds(pl.multiple_of(index * part, part), part)

    started = []
    next_sem = [0]

    def send(src, dst, r, c):
        sem = next_sem[0]
        next_sem[0] += 1
        copy = pltpu.make_async_remote_copy(
            src_ref=src,
            dst_ref=dst,
            send_sem=send_sem.at[sem],
            recv_sem=recv_sem.at[sem],
            device_id={"row": r, "col": c},
            device_id_type=MESH,
        )
        copy.start()
        return copy

    def finish(copies):
        for copy in copies:
            copy.wait_recv()
        started.extend(copies)

    dims = (((1,), (1,)), ((), ()))

    def multiply(left, out, flip):
        deep, wide = left.shape[1], out.shape[1]
        step, span = math.gcd(deep, CHUNK), math.gcd(wide, CHUNK)

        def term(d, w):
            x = left[:, d]
            if flip:
                return lax.dot_general(
                    x, full_hi[w, d], dims, preferred_element_type=jnp.float32
                ) + lax.dot_general(x, full_lo[w, d], dims, preferred_element_type=jnp.float32)
            return jnp.dot(x, full_hi[d, w], preferred_element_type=jnp.float32) + jnp.dot(
                x, full_lo[d, w], preferred_element_type=jnp.float32
            )

        if step == deep and span == wide:
            out[...] = term(slice(None), slice(None)).astype(out.dtype)
            return

        def column(j, carry):
            w = pl.ds(pl.multiple_of(j * span, span), span)

            def add(i, total):
                return total + term(pl.ds(pl.multiple_of(i * step, step), step), w)

            total = lax.fori_loop(0, deep // step, add, jnp.zeros((part, span), jnp.float32))
            out[:, w] = total.astype(out.dtype)
            return carry

        lax.fori_loop(0, wide // span, column, 0)

    def total_of(slots, it, count):
        total = slots[it, 0].astype(jnp.float32)
        for k in range(1, count):
            total = total + slots[it, k].astype(jnp.float32)
        return total

    kind = bound_ref[...].reshape(1, width)
    bounds = (
        cost_ref[...].reshape(1, width),
        jnp.where(kind <= 1, lower_ref[...].reshape(1, width), -jnp.inf),
        jnp.where(kind == 0, upper_ref[...].reshape(1, width), jnp.inf),
    )
    row_kind = jnp.broadcast_to(kind_ref[...].reshape(1, tile), (8, tile)).astype(jnp.float32)
    var_send[...] = jnp.zeros_like(var_send)
    for h in range(2):
        var_send[h, 0:part, 0:width] = primal_ref[h * part : (h + 1) * part, :]
        for place, value in enumerate(bounds):
            var_send[h, part + place : part + place + 1, 0:width] = value
        con_send[h, 0:part] = dual_ref[h * part : (h + 1) * part, :]
        con_send[h, part : 2 * part] = demand_ref[h * part : (h + 1) * part, :]
        con_send[h, 2 * part : 2 * part + 8] = row_kind
    var_recv[me_r] = var_send[half]
    con_recv[:, lanes(me_c)] = con_send[half]
    norm_row[me_r] = jnp.zeros(norm_row.shape[1:], jnp.float32)

    pl.semaphore_wait(barrier, n_row - 1 + 2 * (n_col - 1))

    blocks = [
        send(hi_ref, full_hi.at[rows : 2 * rows], sibling, me_c),
        send(lo_ref, full_lo.at[rows : 2 * rows], sibling, me_c),
    ]
    first_con = []
    for k in range(1, n_col):
        first_con.append(send(con_send.at[half], con_recv.at[:, lanes(me_c)], me_r, col_peer(k)))
    for k in range(n_col):
        first_con.append(
            send(con_send.at[1 - half], con_recv.at[:, lanes(me_c, rows)], sibling, col_peer(k))
        )
    first_var = []
    for k in range(1, n_row):
        peer = row_peer(k)
        first_var.append(send(var_send.at[lax.rem(peer, 2)], var_recv.at[me_r], peer, me_c))
    finish(first_con)
    dual = con_recv[0:part]
    demand = con_recv[part : 2 * part]
    inequality = con_recv[2 * part : 2 * part + 1] == 1.0
    for load in loads:
        load.wait()
    finish(blocks)

    for it in range(ITERS):
        dual_half[...] = dual.astype(jnp.bfloat16)
        multiply(dual_half, back_recv.at[it, chip], False)
        copies = []
        for k in range(1, chips):
            mine = back_recv.at[it, chip]
            copies.append(send(mine, mine, row_peer(2 * k), me_c))
        if it == 0:
            finish(first_var)
            state = jnp.concatenate([var_recv[r, :, 0:width] for r in range(n_row)], axis=1)
            primal = state[0:part]
            cost, lower, upper = (state[part + i : part + i + 1] for i in range(3))
        finish(copies)
        transposed = total_of(back_recv, it, chips)

        moved = primal - PRIMAL_STEP * (cost - transposed)
        moved = jnp.minimum(jnp.maximum(moved, lower), upper)
        point[...] = (2.0 * moved - primal).astype(jnp.bfloat16)
        primal = moved
        multiply(point, fwd_recv.at[it, me_c], True)
        copies = []
        for k in range(1, n_col):
            mine = fwd_recv.at[it, me_c]
            copies.append(send(mine, mine, me_r, col_peer(k)))
        if it == ITERS - 1:
            first = half == 0
            held[...] = primal
            both = held[:, lanes(chip)]
            low, high = both[:, 0:width], both[:, width:]
            fin_send[:, 0:width] = jnp.where(first, high, low)
            fin_send[:, width:] = jnp.zeros((part, tile - width), jnp.float32)
            last = send(fin_send, fin_recv, sibling, me_c)
            primal_out[scens(half), :] = jnp.where(first, low, high)
        finish(copies)
        if it == ITERS - 1:
            finish([last])
            primal_out[scens(1 - half), :] = fin_recv[:, 0:width]
        image = total_of(fwd_recv, it, n_col)

        gap = demand - image
        dual = dual + DUAL_STEP * gap
        dual = jnp.where(inequality, jnp.maximum(dual, 0.0), dual)
        squares = lax.dot_general(
            jnp.ones((8, 2 * rows), jnp.float32),
            gap * gap,
            dims,
            precision=lax.Precision.HIGHEST,
            preferred_element_type=jnp.float32,
        )
        norm_row[me_r, it : it + 1, 0:part] = squares[0:1]

    copies = []
    for k in range(1, n_row):
        mine = norm_row.at[me_r]
        copies.append(send(mine, mine, row_peer(k), me_c))
    held_dual[...] = dual
    last = send(held_dual.at[:, lanes(me_c, rows)], fin_dual, sibling, me_c)
    dual_out[scens(half), :] = held_dual[:, lanes(me_c)]
    finish([last])
    dual_out[scens(1 - half), :] = fin_dual[...]
    finish(copies)
    for h in range(2):
        total = norm_row[h]
        for r in range(h + 2, n_row, 2):
            total = total + norm_row[r]
        norm_out[:, h * part : (h + 1) * part] = jnp.sqrt(
            total[0:ITERS, 0:part] / (n_row * n_col * tile) + NORM_EPS
        )
    for copy in started:
        copy.wait_send()


def shards(
    tile_values,
    tile_row,
    tile_col,
    tile_count,
    primal_init,
    dual_init,
    cost_vector,
    lower_bound,
    upper_bound,
    bound_kind,
    row_kind,
    demand,
):
    n_row = lax.axis_size("row")
    n_col = lax.axis_size("col")
    tile = tile_values.shape[-1]
    scen, width = primal_init.shape
    part = scen // 2
    rows, cols = n_col * tile, (n_row // 2) * tile
    vmem = pl.BlockSpec(memory_space=pltpu.VMEM)
    smem = pl.BlockSpec(memory_space=pltpu.SMEM)
    hbm = pl.BlockSpec(memory_space=pl.ANY)
    half_type = jax.ShapeDtypeStruct((rows, cols), jnp.bfloat16)
    hi, lo = pl.pallas_call(
        dense_kernel,
        out_shape=(half_type, half_type),
        in_specs=[smem, smem, smem, vmem],
        out_specs=(vmem, vmem),
        scratch_shapes=[pltpu.VMEM((rows, cols), jnp.float32)],
        compiler_params=pltpu.CompilerParams(vmem_limit_bytes=VMEM_LIMIT),
    )(tile_row, tile_col, tile_count, tile_values)
    chips = n_row // 2
    sems = ITERS * (chips + n_col) + 2 * (n_row + n_col) + 8
    f32, bf16 = jnp.float32, jnp.bfloat16
    return pl.pallas_call(
        functools.partial(step_kernel, n_row, n_col),
        out_shape=(
            jax.ShapeDtypeStruct((scen, width), f32),
            jax.ShapeDtypeStruct((scen, tile), f32),
            jax.ShapeDtypeStruct((ITERS, scen), f32),
        ),
        in_specs=[hbm, hbm] + [vmem] * 8,
        out_specs=(vmem, vmem, vmem),
        scratch_shapes=[
            pltpu.VMEM((2 * rows, cols), bf16),
            pltpu.VMEM((2 * rows, cols), bf16),
            pltpu.VMEM((2, part + 8, tile), f32),
            pltpu.VMEM((n_row, part + 8, tile), f32),
            pltpu.VMEM((2, 2 * part + 8, tile), f32),
            pltpu.VMEM((2 * part + 8, 2 * rows), f32),
            pltpu.VMEM((part, 2 * rows), bf16),
            pltpu.VMEM((part, cols), bf16),
            pltpu.VMEM((ITERS, chips, part, cols), BACK_TYPE),
            pltpu.VMEM((ITERS, n_col, part, 2 * rows), FWD_TYPE),
            pltpu.VMEM((part, cols), f32),
            pltpu.VMEM((part, 2 * rows), f32),
            pltpu.VMEM((part, tile), f32),
            pltpu.VMEM((part, tile), f32),
            pltpu.VMEM((part, tile), f32),
            pltpu.VMEM((n_row, 8, tile), f32),
            pltpu.SemaphoreType.DMA((2,)),
            pltpu.SemaphoreType.DMA((sems,)),
            pltpu.SemaphoreType.DMA((sems,)),
        ],
        compiler_params=pltpu.CompilerParams(
            collective_id=0, has_side_effects=True, vmem_limit_bytes=VMEM_LIMIT
        ),
    )(
        hi,
        lo,
        primal_init,
        dual_init,
        cost_vector,
        lower_bound,
        upper_bound,
        bound_kind,
        row_kind,
        demand,
    )


def solution(mesh):
    return jax.shard_map(
        shards,
        mesh=mesh,
        in_specs=(
            P("row", "col", None, None, None),
            P("row", "col", None),
            P("row", "col", None),
            P("row", "col"),
            P(None, ("row", "col")),
            P(None, ("row", "col")),
            P(("row", "col")),
            P(("row", "col")),
            P(("row", "col")),
            P(("row", "col")),
            P(("row", "col")),
            P(None, ("row", "col")),
        ),
        out_specs=(P(None, ("row", "col")), P(None, ("row", "col")), P()),
        check_vma=False,
    )
```

```python
import functools
import math

import jax
import jax.numpy as jnp
from jax import lax
from jax.experimental import pallas as pl
from jax.experimental.pallas import tpu as pltpu
from jax.sharding import PartitionSpec as P

ITERS = 3
PRIMAL_STEP = 0.4
DUAL_STEP = 0.4
NORM_EPS = 1e-06
MESH = pl.DeviceIdType.MESH
CHUNK = 1024
BACK_TYPE = jnp.bfloat16
FWD_TYPE = jnp.bfloat16
VMEM_LIMIT = 56 * 1024 * 1024


def dense_kernel(rows_ref, cols_ref, count_ref, tiles_ref, hi_ref, lo_ref, acc):
    tile = tiles_ref.shape[-1]
    acc[...] = jnp.zeros_like(acc)

    def add(slot, carry):
        r = pl.multiple_of(rows_ref[0, 0, slot] * tile, tile)
        c = pl.multiple_of(cols_ref[0, 0, slot] * tile, tile)
        where = (pl.ds(r, tile), pl.ds(c, tile))
        acc[where] += tiles_ref[0, 0, slot].astype(jnp.float32)
        return carry

    lax.fori_loop(0, count_ref[0, 0], add, 0)

    def split(block, carry):
        where = (pl.ds(pl.multiple_of(block * tile, tile), tile), slice(None))
        whole = acc[where]
        hi = whole.astype(jnp.bfloat16)
        hi_ref[where] = hi
        lo_ref[where] = (whole - hi.astype(jnp.float32)).astype(jnp.bfloat16)
        return carry

    lax.fori_loop(0, acc.shape[0] // tile, split, 0)


def step_kernel(
    n_row,
    n_col,
    hi_ref,
    lo_ref,
    primal_ref,
    dual_ref,
    cost_ref,
    lower_ref,
    upper_ref,
    bound_ref,
    kind_ref,
    demand_ref,
    primal_out,
    dual_out,
    norm_out,
    full_hi,
    full_lo,
    var_send,
    var_recv,
    con_send,
    con_recv,
    dual_half,
    point,
    back_recv,
    fwd_recv,
    held,
    held_dual,
    fin_send,
    fin_recv,
    fin_dual,
    norm_row,
    local_sem,
    send_sem,
    recv_sem,
):
    me_r = lax.axis_index("row")
    me_c = lax.axis_index("col")
    chips = n_row // 2
    chip = me_r // 2
    half = lax.rem(me_r, 2)
    scen, tile = dual_ref.shape
    part = scen // 2
    width = primal_ref.shape[1]
    rows, cols = hi_ref.shape
    sibling = me_r + 1 - 2 * half

    def row_peer(k):
        return lax.rem(me_r + k, n_row)

    def col_peer(k):
        return lax.rem(me_c + k, n_col)

    barrier = pltpu.get_barrier_semaphore()
    for k in range(1, n_row):
        pl.semaphore_signal(
            barrier, inc=1, device_id={"row": row_peer(k), "col": me_c}, device_id_type=MESH
        )
    for k in range(1, n_col):
        for r in (me_r, sibling):
            pl.semaphore_signal(
                barrier, inc=1, device_id={"row": r, "col": col_peer(k)}, device_id_type=MESH
            )
    loads = [
        pltpu.make_async_copy(hi_ref, full_hi.at[0:rows], local_sem.at[0]),
        pltpu.make_async_copy(lo_ref, full_lo.at[0:rows], local_sem.at[1]),
    ]
    for load in loads:
        load.start()

    def lanes(index, offset=0):
        return pl.ds(pl.multiple_of(index * tile + offset, tile), tile)

    def scens(index):
        return pl.ds(pl.multiple_of(index * part, part), part)

    started = []
    next_sem = [0]

    def send(src, dst, r, c):
        sem = next_sem[0]
        next_sem[0] += 1
        copy = pltpu.make_async_remote_copy(
            src_ref=src,
            dst_ref=dst,
            send_sem=send_sem.at[sem],
            recv_sem=recv_sem.at[sem],
            device_id={"row": r, "col": c},
            device_id_type=MESH,
        )
        copy.start()
        return copy

    def finish(copies):
        for copy in copies:
            copy.wait_recv()
        started.extend(copies)

    dims = (((1,), (1,)), ((), ()))

    def multiply(left, out, flip, base=0):
        deep, wide = left.shape[1], out.shape[1]
        step, span = math.gcd(deep, CHUNK), math.gcd(wide, CHUNK)
        matrix_hi = full_hi.at[pl.ds(base, wide)] if flip else full_hi
        matrix_lo = full_lo.at[pl.ds(base, wide)] if flip else full_lo

        def term(d, w):
            x = left[:, d]
            if flip:
                return lax.dot_general(
                    x, matrix_hi[w, d], dims, preferred_element_type=jnp.float32
                ) + lax.dot_general(x, matrix_lo[w, d], dims, preferred_element_type=jnp.float32)
            return jnp.dot(x, matrix_hi[d, w], preferred_element_type=jnp.float32) + jnp.dot(
                x, matrix_lo[d, w], preferred_element_type=jnp.float32
            )

        if step == deep and span == wide:
            out[...] = term(slice(None), slice(None)).astype(out.dtype)
            return

        def column(j, carry):
            w = pl.ds(pl.multiple_of(j * span, span), span)

            def add(i, total):
                return total + term(pl.ds(pl.multiple_of(i * step, step), step), w)

            total = lax.fori_loop(0, deep // step, add, jnp.zeros((part, span), jnp.float32))
            out[:, w] = total.astype(out.dtype)
            return carry

        lax.fori_loop(0, wide // span, column, 0)

    def total_of(slots, it, count):
        total = slots[it, 0].astype(jnp.float32)
        for k in range(1, count):
            total = total + slots[it, k].astype(jnp.float32)
        return total

    kind = bound_ref[...].reshape(1, width)
    bounds = (
        cost_ref[...].reshape(1, width),
        jnp.where(kind <= 1, lower_ref[...].reshape(1, width), -jnp.inf),
        jnp.where(kind == 0, upper_ref[...].reshape(1, width), jnp.inf),
    )
    row_kind = jnp.broadcast_to(kind_ref[...].reshape(1, tile), (8, tile)).astype(jnp.float32)
    var_send[...] = jnp.zeros_like(var_send)
    for h in range(2):
        var_send[h, 0:part, 0:width] = primal_ref[h * part : (h + 1) * part, :]
        for place, value in enumerate(bounds):
            var_send[h, part + place : part + place + 1, 0:width] = value
        con_send[h, 0:part] = dual_ref[h * part : (h + 1) * part, :]
        con_send[h, part : 2 * part] = demand_ref[h * part : (h + 1) * part, :]
        con_send[h, 2 * part : 2 * part + 8] = row_kind
    var_recv[me_r] = var_send[half]
    con_recv[:, lanes(me_c)] = con_send[half]
    norm_row[me_r] = jnp.zeros(norm_row.shape[1:], jnp.float32)

    pl.semaphore_wait(barrier, n_row - 1 + 2 * (n_col - 1))

    blocks = [
        send(hi_ref, full_hi.at[rows : 2 * rows], sibling, me_c),
        send(lo_ref, full_lo.at[rows : 2 * rows], sibling, me_c),
    ]
    first_con = []
    for k in range(1, n_col):
        first_con.append(send(con_send.at[half], con_recv.at[:, lanes(me_c)], me_r, col_peer(k)))
    for k in range(n_col):
        first_con.append(
            send(con_send.at[1 - half], con_recv.at[:, lanes(me_c, rows)], sibling, col_peer(k))
        )
    first_var = []
    for k in range(1, n_row):
        peer = row_peer(k)
        first_var.append(send(var_send.at[lax.rem(peer, 2)], var_recv.at[me_r], peer, me_c))
    finish(first_con)
    dual = con_recv[0:part]
    demand = con_recv[part : 2 * part]
    inequality = con_recv[2 * part : 2 * part + 1] == 1.0
    for load in loads:
        load.wait()
    finish(blocks)

    for it in range(ITERS):
        dual_half[...] = dual.astype(jnp.bfloat16)
        multiply(dual_half, back_recv.at[it, chip], False)
        copies = []
        for k in range(1, chips):
            mine = back_recv.at[it, chip]
            copies.append(send(mine, mine, row_peer(2 * k), me_c))
        if it == 0:
            finish(first_var)
            state = jnp.concatenate([var_recv[r, :, 0:width] for r in range(n_row)], axis=1)
            primal = state[0:part]
            cost, lower, upper = (state[part + i : part + i + 1] for i in range(3))
        finish(copies)
        transposed = total_of(back_recv, it, chips)

        moved = primal - PRIMAL_STEP * (cost - transposed)
        moved = jnp.minimum(jnp.maximum(moved, lower), upper)
        point[...] = (2.0 * moved - primal).astype(jnp.bfloat16)
        primal = moved
        copies = []
        for group in range(2):
            mine = fwd_recv.at[it, me_c, :, group * rows : (group + 1) * rows]
            multiply(point, mine, True, group * rows)
            for k in range(1, n_col):
                copies.append(send(mine, mine, me_r, col_peer(k)))
        if it == ITERS - 1:
            first = half == 0
            held[...] = primal
            both = held[:, lanes(chip)]
            low, high = both[:, 0:width], both[:, width:]
            fin_send[:, 0:width] = jnp.where(first, high, low)
            fin_send[:, width:] = jnp.zeros((part, tile - width), jnp.float32)
            last = send(fin_send, fin_recv, sibling, me_c)
            primal_out[scens(half), :] = jnp.where(first, low, high)
        finish(copies)
        if it == ITERS - 1:
            finish([last])
            primal_out[scens(1 - half), :] = fin_recv[:, 0:width]
        image = total_of(fwd_recv, it, n_col)

        gap = demand - image
        dual = dual + DUAL_STEP * gap
        dual = jnp.where(inequality, jnp.maximum(dual, 0.0), dual)
        squares = lax.dot_general(
            jnp.ones((8, 2 * rows), jnp.float32),
            gap * gap,
            dims,
            precision=lax.Precision.HIGHEST,
            preferred_element_type=jnp.float32,
        )
        norm_row[me_r, it : it + 1, 0:part] = squares[0:1]

    copies = []
    for k in range(1, n_row):
        mine = norm_row.at[me_r]
        copies.append(send(mine, mine, row_peer(k), me_c))
    held_dual[...] = dual
    last = send(held_dual.at[:, lanes(me_c, rows)], fin_dual, sibling, me_c)
    dual_out[scens(half), :] = held_dual[:, lanes(me_c)]
    finish([last])
    dual_out[scens(1 - half), :] = fin_dual[...]
    finish(copies)
    for h in range(2):
        total = norm_row[h]
        for r in range(h + 2, n_row, 2):
            total = total + norm_row[r]
        norm_out[:, h * part : (h + 1) * part] = jnp.sqrt(
            total[0:ITERS, 0:part] / (n_row * n_col * tile) + NORM_EPS
        )
    for copy in started:
        copy.wait_send()


def tail_kernel(primal_ref, dual_ref, norm_ref, primal_out, dual_out, norm_out):
    primal_out[...] = primal_ref[...]
    dual_out[...] = dual_ref[...]
    norm_out[...] = norm_ref[...]


def shards(
    tile_values,
    tile_row,
    tile_col,
    tile_count,
    primal_init,
    dual_init,
    cost_vector,
    lower_bound,
    upper_bound,
    bound_kind,
    row_kind,
    demand,
):
    n_row = lax.axis_size("row")
    n_col = lax.axis_size("col")
    tile = tile_values.shape[-1]
    scen, width = primal_init.shape
    part = scen // 2
    rows, cols = n_col * tile, (n_row // 2) * tile
    vmem = pl.BlockSpec(memory_space=pltpu.VMEM)
    smem = pl.BlockSpec(memory_space=pltpu.SMEM)
    hbm = pl.BlockSpec(memory_space=pl.ANY)
    half_type = jax.ShapeDtypeStruct((rows, cols), jnp.bfloat16)
    hi, lo = pl.pallas_call(
        dense_kernel,
        out_shape=(half_type, half_type),
        in_specs=[smem, smem, smem, vmem],
        out_specs=(vmem, vmem),
        scratch_shapes=[pltpu.VMEM((rows, cols), jnp.float32)],
        compiler_params=pltpu.CompilerParams(vmem_limit_bytes=VMEM_LIMIT),
    )(tile_row, tile_col, tile_count, tile_values)
    chips = n_row // 2
    sems = ITERS * (chips + 2 * n_col) + 2 * (n_row + n_col) + 8
    f32, bf16 = jnp.float32, jnp.bfloat16
    outs = (
        jax.ShapeDtypeStruct((scen, width), f32),
        jax.ShapeDtypeStruct((scen, tile), f32),
        jax.ShapeDtypeStruct((ITERS, scen), f32),
    )
    results = pl.pallas_call(
        functools.partial(step_kernel, n_row, n_col),
        out_shape=outs,
        in_specs=[hbm, hbm] + [vmem] * 8,
        out_specs=(vmem, vmem, vmem),
        scratch_shapes=[
            pltpu.VMEM((2 * rows, cols), bf16),
            pltpu.VMEM((2 * rows, cols), bf16),
            pltpu.VMEM((2, part + 8, tile), f32),
            pltpu.VMEM((n_row, part + 8, tile), f32),
            pltpu.VMEM((2, 2 * part + 8, tile), f32),
            pltpu.VMEM((2 * part + 8, 2 * rows), f32),
            pltpu.VMEM((part, 2 * rows), bf16),
            pltpu.VMEM((part, cols), bf16),
            pltpu.VMEM((ITERS, chips, part, cols), BACK_TYPE),
            pltpu.VMEM((ITERS, n_col, part, 2 * rows), FWD_TYPE),
            pltpu.VMEM((part, cols), f32),
            pltpu.VMEM((part, 2 * rows), f32),
            pltpu.VMEM((part, tile), f32),
            pltpu.VMEM((part, tile), f32),
            pltpu.VMEM((part, tile), f32),
            pltpu.VMEM((n_row, 8, tile), f32),
            pltpu.SemaphoreType.DMA((2,)),
            pltpu.SemaphoreType.DMA((sems,)),
            pltpu.SemaphoreType.DMA((sems,)),
        ],
        compiler_params=pltpu.CompilerParams(
            collective_id=0, has_side_effects=True, vmem_limit_bytes=VMEM_LIMIT
        ),
    )(
        hi,
        lo,
        primal_init,
        dual_init,
        cost_vector,
        lower_bound,
        upper_bound,
        bound_kind,
        row_kind,
        demand,
    )
    return pl.pallas_call(
        tail_kernel, out_shape=outs, in_specs=[vmem] * 3, out_specs=(vmem, vmem, vmem)
    )(*results)


def solution(mesh):
    return jax.shard_map(
        shards,
        mesh=mesh,
        in_specs=(
            P("row", "col", None, None, None),
            P("row", "col", None),
            P("row", "col", None),
            P("row", "col"),
            P(None, ("row", "col")),
            P(None, ("row", "col")),
            P(("row", "col")),
            P(("row", "col")),
            P(("row", "col")),
            P(("row", "col")),
            P(("row", "col")),
            P(None, ("row", "col")),
        ),
        out_specs=(P(None, ("row", "col")), P(None, ("row", "col")), P()),
        check_vma=False,
    )
```

```python
import functools
import math

import jax
import jax.numpy as jnp
from jax import lax
from jax.experimental import pallas as pl
from jax.experimental.pallas import tpu as pltpu
from jax.sharding import PartitionSpec as P

ITERS = 3
PRIMAL_STEP = 0.4
DUAL_STEP = 0.4
NORM_EPS = 1e-06
MESH = pl.DeviceIdType.MESH
CHUNK = 1024
BACK_TYPE = jnp.bfloat16
FWD_TYPE = jnp.bfloat16
VMEM_LIMIT = 56 * 1024 * 1024


def dense_kernel(rows_ref, cols_ref, count_ref, tiles_ref, hi_ref, lo_ref, acc):
    tile = tiles_ref.shape[-1]
    acc[...] = jnp.zeros_like(acc)

    def add(slot, carry):
        r = pl.multiple_of(rows_ref[0, 0, slot] * tile, tile)
        c = pl.multiple_of(cols_ref[0, 0, slot] * tile, tile)
        where = (pl.ds(r, tile), pl.ds(c, tile))
        acc[where] += tiles_ref[0, 0, slot].astype(jnp.float32)
        return carry

    lax.fori_loop(0, count_ref[0, 0], add, 0)

    def split(block, carry):
        where = (pl.ds(pl.multiple_of(block * tile, tile), tile), slice(None))
        whole = acc[where]
        hi = whole.astype(jnp.bfloat16)
        hi_ref[where] = hi
        lo_ref[where] = (whole - hi.astype(jnp.float32)).astype(jnp.bfloat16)
        return carry

    lax.fori_loop(0, acc.shape[0] // tile, split, 0)


def step_kernel(
    n_row,
    n_col,
    hi_ref,
    lo_ref,
    primal_ref,
    dual_ref,
    cost_ref,
    lower_ref,
    upper_ref,
    bound_ref,
    kind_ref,
    demand_ref,
    primal_out,
    dual_out,
    norm_out,
    full_hi,
    full_lo,
    var_send,
    var_recv,
    con_send,
    con_recv,
    dual_half,
    point,
    back_recv,
    fwd_recv,
    held,
    held_dual,
    fin_send,
    fin_recv,
    fin_dual,
    norm_row,
    local_sem,
    send_sem,
    recv_sem,
):
    me_r = lax.axis_index("row")
    me_c = lax.axis_index("col")
    chips = n_row // 2
    chip = me_r // 2
    half = lax.rem(me_r, 2)
    scen, tile = dual_ref.shape
    part = scen // 2
    width = primal_ref.shape[1]
    rows, cols = hi_ref.shape
    sibling = me_r + 1 - 2 * half

    def row_peer(k):
        return lax.rem(me_r + k, n_row)

    def col_peer(k):
        return lax.rem(me_c + k, n_col)

    barrier = pltpu.get_barrier_semaphore()
    for k in range(1, n_row):
        pl.semaphore_signal(
            barrier, inc=1, device_id={"row": row_peer(k), "col": me_c}, device_id_type=MESH
        )
    for k in range(1, n_col):
        for r in (me_r, sibling):
            pl.semaphore_signal(
                barrier, inc=1, device_id={"row": r, "col": col_peer(k)}, device_id_type=MESH
            )
    loads = [
        pltpu.make_async_copy(hi_ref, full_hi.at[0:rows], local_sem.at[0]),
        pltpu.make_async_copy(lo_ref, full_lo.at[0:rows], local_sem.at[1]),
    ]
    for load in loads:
        load.start()

    def lanes(index, offset=0):
        return pl.ds(pl.multiple_of(index * tile + offset, tile), tile)

    def scens(index):
        return pl.ds(pl.multiple_of(index * part, part), part)

    started = []
    next_sem = [0]

    def send(src, dst, r, c):
        sem = next_sem[0]
        next_sem[0] += 1
        copy = pltpu.make_async_remote_copy(
            src_ref=src,
            dst_ref=dst,
            send_sem=send_sem.at[sem],
            recv_sem=recv_sem.at[sem],
            device_id={"row": r, "col": c},
            device_id_type=MESH,
        )
        copy.start()
        return copy

    def finish(copies):
        for copy in copies:
            copy.wait_recv()
        started.extend(copies)

    dims = (((1,), (1,)), ((), ()))

    def multiply(left, out, flip, base=0):
        deep, wide = left.shape[1], out.shape[1]
        step, span = math.gcd(deep, CHUNK), math.gcd(wide, CHUNK)
        matrix_hi = full_hi.at[pl.ds(base, wide)] if flip else full_hi
        matrix_lo = full_lo.at[pl.ds(base, wide)] if flip else full_lo

        def term(d, w):
            x = left[:, d]
            if flip:
                return lax.dot_general(
                    x, matrix_hi[w, d], dims, preferred_element_type=jnp.float32
                ) + lax.dot_general(x, matrix_lo[w, d], dims, preferred_element_type=jnp.float32)
            return jnp.dot(x, matrix_hi[d, w], preferred_element_type=jnp.float32) + jnp.dot(
                x, matrix_lo[d, w], preferred_element_type=jnp.float32
            )

        if step == deep and span == wide:
            out[...] = term(slice(None), slice(None)).astype(out.dtype)
            return

        def column(j, carry):
            w = pl.ds(pl.multiple_of(j * span, span), span)

            def add(i, total):
                return total + term(pl.ds(pl.multiple_of(i * step, step), step), w)

            total = lax.fori_loop(0, deep // step, add, jnp.zeros((left.shape[0], span), jnp.float32))
            out[:, w] = total.astype(out.dtype)
            return carry

        lax.fori_loop(0, wide // span, column, 0)

    def total_of(slots, it, count, span):
        total = slots[it, 0, span].astype(jnp.float32)
        for k in range(1, count):
            total = total + slots[it, k, span].astype(jnp.float32)
        return total

    kind = bound_ref[...].reshape(1, width)
    bounds = (
        cost_ref[...].reshape(1, width),
        jnp.where(kind <= 1, lower_ref[...].reshape(1, width), -jnp.inf),
        jnp.where(kind == 0, upper_ref[...].reshape(1, width), jnp.inf),
    )
    row_kind = jnp.broadcast_to(kind_ref[...].reshape(1, tile), (8, tile)).astype(jnp.float32)
    var_send[...] = jnp.zeros_like(var_send)
    for h in range(2):
        var_send[h, 0:part, 0:width] = primal_ref[h * part : (h + 1) * part, :]
        for place, value in enumerate(bounds):
            var_send[h, part + place : part + place + 1, 0:width] = value
        con_send[h, 0:part] = dual_ref[h * part : (h + 1) * part, :]
        con_send[h, part : 2 * part] = demand_ref[h * part : (h + 1) * part, :]
        con_send[h, 2 * part : 2 * part + 8] = row_kind
    var_recv[me_r] = var_send[half]
    con_recv[:, lanes(me_c)] = con_send[half]
    norm_row[me_r] = jnp.zeros(norm_row.shape[1:], jnp.float32)

    pl.semaphore_wait(barrier, n_row - 1 + 2 * (n_col - 1))

    first_con = []
    for k in range(1, n_col):
        first_con.append(send(con_send.at[half], con_recv.at[:, lanes(me_c)], me_r, col_peer(k)))
    for k in range(n_col):
        first_con.append(
            send(con_send.at[1 - half], con_recv.at[:, lanes(me_c, rows)], sibling, col_peer(k))
        )
    blocks = [
        send(hi_ref, full_hi.at[rows : 2 * rows], sibling, me_c),
        send(lo_ref, full_lo.at[rows : 2 * rows], sibling, me_c),
    ]
    first_var = []
    for k in range(1, n_row):
        peer = row_peer(k)
        first_var.append(send(var_send.at[lax.rem(peer, 2)], var_recv.at[me_r], peer, me_c))
    finish(first_con)
    dual = con_recv[0:part]
    demand = con_recv[part : 2 * part]
    inequality = con_recv[2 * part : 2 * part + 1] == 1.0
    for load in loads:
        load.wait()
    finish(blocks)

    gaps = []

    def settle(it, g):
        gap = demand[spans[g]] - total_of(fwd_recv, it, n_col, spans[g])
        moved = dual_parts[g] + DUAL_STEP * gap
        dual_parts[g] = jnp.where(inequality, jnp.maximum(moved, 0.0), moved)
        gaps.append(gap)

    def square(it):
        gap = jnp.concatenate(gaps[2 * it : 2 * it + 2], axis=0)
        squares = lax.dot_general(
            jnp.ones((8, 2 * rows), jnp.float32),
            gap * gap,
            dims,
            precision=lax.Precision.HIGHEST,
            preferred_element_type=jnp.float32,
        )
        norm_row[me_r, it : it + 1, 0:part] = squares[0:1]

    group = part // 2
    spans = [slice(g * group, (g + 1) * group) for g in range(2)]
    dual_parts = [dual[span] for span in spans]
    primal_parts = [None, None]
    for it in range(ITERS):
        flights = []
        for g, span in enumerate(spans):
            if it > 0:
                finish(arriving[g])
                settle(it - 1, g)
            dual_half[span] = dual_parts[g].astype(jnp.bfloat16)
            mine = back_recv.at[it, chip, span]
            multiply(dual_half.at[span], mine, False)
            flights.append([send(mine, mine, row_peer(2 * k), me_c) for k in range(1, chips)])
        if it == 0:
            finish(first_var)
            state = jnp.concatenate([var_recv[r, :, 0:width] for r in range(n_row)], axis=1)
            primal_parts = [state[span] for span in spans]
            cost, lower, upper = (state[part + i : part + i + 1] for i in range(3))
        else:
            square(it - 1)
        arriving = []
        for g, span in enumerate(spans):
            finish(flights[g])
            transposed = total_of(back_recv, it, chips, span)
            primal = primal_parts[g]
            moved = primal - PRIMAL_STEP * (cost - transposed)
            moved = jnp.minimum(jnp.maximum(moved, lower), upper)
            point[span] = (2.0 * moved - primal).astype(jnp.bfloat16)
            primal_parts[g] = moved
            mine = fwd_recv.at[it, me_c, span]
            multiply(point.at[span], mine, True)
            arriving.append([send(mine, mine, me_r, col_peer(k)) for k in range(1, n_col)])
    first = half == 0
    for g, span in enumerate(spans):
        held[span] = primal_parts[g]
    both = held[:, lanes(chip)]
    low, high = both[:, 0:width], both[:, width:]
    fin_send[:, 0:width] = jnp.where(first, high, low)
    fin_send[:, width:] = jnp.zeros((part, tile - width), jnp.float32)
    last = send(fin_send, fin_recv, sibling, me_c)
    primal_out[scens(half), :] = jnp.where(first, low, high)
    for g in range(2):
        finish(arriving[g])
        settle(ITERS - 1, g)
    finish([last])
    primal_out[scens(1 - half), :] = fin_recv[:, 0:width]
    dual = jnp.concatenate(dual_parts, axis=0)
    square(ITERS - 1)
    copies = []
    for k in range(1, n_row):
        mine = norm_row.at[me_r]
        copies.append(send(mine, mine, row_peer(k), me_c))
    held_dual[...] = dual
    last = send(held_dual.at[:, lanes(me_c, rows)], fin_dual, sibling, me_c)
    dual_out[scens(half), :] = held_dual[:, lanes(me_c)]
    finish([last])
    dual_out[scens(1 - half), :] = fin_dual[...]
    finish(copies)
    for h in range(2):
        total = norm_row[h]
        for r in range(h + 2, n_row, 2):
            total = total + norm_row[r]
        norm_out[:, h * part : (h + 1) * part] = jnp.sqrt(
            total[0:ITERS, 0:part] / (n_row * n_col * tile) + NORM_EPS
        )
    for copy in started:
        copy.wait_send()


def tail_kernel(primal_ref, dual_ref, norm_ref, primal_out, dual_out, norm_out):
    primal_out[...] = primal_ref[...]
    dual_out[...] = dual_ref[...]
    norm_out[...] = norm_ref[...]


def shards(
    tile_values,
    tile_row,
    tile_col,
    tile_count,
    primal_init,
    dual_init,
    cost_vector,
    lower_bound,
    upper_bound,
    bound_kind,
    row_kind,
    demand,
):
    n_row = lax.axis_size("row")
    n_col = lax.axis_size("col")
    tile = tile_values.shape[-1]
    scen, width = primal_init.shape
    part = scen // 2
    rows, cols = n_col * tile, (n_row // 2) * tile
    vmem = pl.BlockSpec(memory_space=pltpu.VMEM)
    smem = pl.BlockSpec(memory_space=pltpu.SMEM)
    hbm = pl.BlockSpec(memory_space=pl.ANY)
    half_type = jax.ShapeDtypeStruct((rows, cols), jnp.bfloat16)
    hi, lo = pl.pallas_call(
        dense_kernel,
        out_shape=(half_type, half_type),
        in_specs=[smem, smem, smem, vmem],
        out_specs=(vmem, vmem),
        scratch_shapes=[pltpu.VMEM((rows, cols), jnp.float32)],
        compiler_params=pltpu.CompilerParams(vmem_limit_bytes=VMEM_LIMIT),
    )(tile_row, tile_col, tile_count, tile_values)
    chips = n_row // 2
    sems = ITERS * 2 * (chips + n_col) + 2 * (n_row + n_col) + 8
    f32, bf16 = jnp.float32, jnp.bfloat16
    outs = (
        jax.ShapeDtypeStruct((scen, width), f32),
        jax.ShapeDtypeStruct((scen, tile), f32),
        jax.ShapeDtypeStruct((ITERS, scen), f32),
    )
    results = pl.pallas_call(
        functools.partial(step_kernel, n_row, n_col),
        out_shape=outs,
        in_specs=[hbm, hbm] + [vmem] * 8,
        out_specs=(vmem, vmem, vmem),
        scratch_shapes=[
            pltpu.VMEM((2 * rows, cols), bf16),
            pltpu.VMEM((2 * rows, cols), bf16),
            pltpu.VMEM((2, part + 8, tile), f32),
            pltpu.VMEM((n_row, part + 8, tile), f32),
            pltpu.VMEM((2, 2 * part + 8, tile), f32),
            pltpu.VMEM((2 * part + 8, 2 * rows), f32),
            pltpu.VMEM((part, 2 * rows), bf16),
            pltpu.VMEM((part, cols), bf16),
            pltpu.VMEM((ITERS, chips, part, cols), BACK_TYPE),
            pltpu.VMEM((ITERS, n_col, part, 2 * rows), FWD_TYPE),
            pltpu.VMEM((part, cols), f32),
            pltpu.VMEM((part, 2 * rows), f32),
            pltpu.VMEM((part, tile), f32),
            pltpu.VMEM((part, tile), f32),
            pltpu.VMEM((part, tile), f32),
            pltpu.VMEM((n_row, 8, tile), f32),
            pltpu.SemaphoreType.DMA((2,)),
            pltpu.SemaphoreType.DMA((sems,)),
            pltpu.SemaphoreType.DMA((sems,)),
        ],
        compiler_params=pltpu.CompilerParams(
            collective_id=0, has_side_effects=True, vmem_limit_bytes=VMEM_LIMIT
        ),
    )(
        hi,
        lo,
        primal_init,
        dual_init,
        cost_vector,
        lower_bound,
        upper_bound,
        bound_kind,
        row_kind,
        demand,
    )
    return pl.pallas_call(
        tail_kernel, out_shape=outs, in_specs=[vmem] * 3, out_specs=(vmem, vmem, vmem)
    )(*results)


def solution(mesh):
    return jax.shard_map(
        shards,
        mesh=mesh,
        in_specs=(
            P("row", "col", None, None, None),
            P("row", "col", None),
            P("row", "col", None),
            P("row", "col"),
            P(None, ("row", "col")),
            P(None, ("row", "col")),
            P(("row", "col")),
            P(("row", "col")),
            P(("row", "col")),
            P(("row", "col")),
            P(("row", "col")),
            P(None, ("row", "col")),
        ),
        out_specs=(P(None, ("row", "col")), P(None, ("row", "col")), P()),
        check_vma=False,
    )
```
